32 devices in a mesh: gx: 4 (over y, x), gy: 8 (over z, core).
Axes of the slice: x: 2, y: 2, z: 4, core: 2. Of those that a mesh axis runs over, the one named last changes fastest.
Arguments:
- features: bfloat16 [32768, 768], P(('gx', 'gy')), may hold values from -6 to 6
- seed_rows: int32 [2048], P(('gx', 'gy')), may hold values from 0 to 1023
- hop1_ids: int32 [2048, 5], P(('gx', 'gy')), may hold values from 0 to 32767, as said below
- hop2_ids: int32 [2048, 5, 5], P(('gx', 'gy')), may hold values from 0 to 32767, as said below
- w_self: bfloat16 [768, 1024], replicated, may hold values from -0.21875 to 0.21875
- w_neigh: bfloat16 [768, 1024], replicated, may hold values from -0.21875 to 0.21875
- bias: float32 [1024], replicated, may hold values from -3 to 3
- cotangent: bfloat16 [2048, 1024], P(('gx', 'gy')), may hold values from -6 to 6
Outputs:
- embedded: bfloat16 [2048, 1024], P(('gx', 'gy'))
- grad_self: float32 [768, 1024], P(None, ('gx', 'gy'))
- grad_neigh: float32 [768, 1024], P(None, ('gx', 'gy'))
- grad_bias: float32 [1024], P(('gx', 'gy'))
The draws below stay inside these ranges and needn't reach their ends.
Inputs may be any that keep to these rules, and one draw needn't show every extreme that they name: `hop1_ids`: row i belongs to device i // 1024 (device index gx * 8 + gy). The 320 entries of one device name at most 15 rows of any one owner, repeats counted; in every draw one owner receives exactly 15 from every device. `hop2_ids`: row i belongs to device i // 1024. The 1600 entries of one device name at most 75 rows of any one owner, repeats counted; in every draw one owner receives exactly 75 from every device.
All inputs are finite; a program needn't handle non-finite values.
Results may differ from the reference program's by a relative error of at most 0.025.
The reference program's roundings to bfloat16 on the way (of `x_seed`, `x_near`, `pooled_far`, `hidden_near`, `pooled_near`, `hidden_seed` and `spread`) count: a program that leaves them out, or rounds other values in their place, can miss the bound.
Values may be sent and summed in bfloat16 or wider, within the bound.
A program may use at most 64 MiB of HBM per device.

```python
import jax
import jax.numpy as jnp
from jax import lax

F = 768
H = 1024
SEEDS = 64
ROWS_DEV = 1024
K1 = 5
K2 = 5
NODES = 32768
SEEDS_ALL = 2048
CAP1 = 15
CAP2 = 75
N_GX = 4
N_GY = 8


def plan_owners(key, item_count, capacity):
    devices = N_GX * N_GY
    hot_owner = jax.random.randint(jax.random.fold_in(key, 7), (), 0, devices)
    device_keys = jax.random.split(jax.random.fold_in(key, 11), devices)

    def per_device(device_key):
        key_perm, key_shuffle, key_rows = jax.random.split(device_key, 3)
        shuffled = jax.random.permutation(key_perm, devices * capacity)
        priority = jnp.where(shuffled // capacity == hot_owner, 0, 1 + jnp.arange(devices * capacity))
        chosen = shuffled[jnp.argsort(priority, stable=True)][:item_count]
        chosen = chosen[jax.random.permutation(key_shuffle, item_count)]
        owners = chosen // capacity
        row_ids = jax.random.randint(key_rows, (item_count,), 0, ROWS_DEV)
        return (owners * ROWS_DEV + row_ids).astype(jnp.int32)
    return jax.vmap(per_device)(device_keys)


def draw_hop1_ids(key, part):
    picked = plan_owners(jax.random.fold_in(key, 101), SEEDS * K1, CAP1)
    return picked.reshape(SEEDS_ALL, K1).astype(jnp.int32)


def draw_hop2_ids(key, part):
    picked = plan_owners(jax.random.fold_in(key, 202), SEEDS * K1 * K2, CAP2)
    return picked.reshape(SEEDS_ALL, K1, K2).astype(jnp.int32)


def place_ends(values, stream_key, smallest, largest):
    longest = values.shape.index(max(values.shape))
    spots = []
    for shift in (0, 1):
        where = [jax.random.randint(jax.random.fold_in(stream_key, axis), (), 0, length) for axis, length in enumerate(values.shape)]
        where[longest] = (where[longest] + shift) % values.shape[longest]
        spots.append(tuple(where))
    return values.at[spots[0]].set(smallest).at[spots[1]].set(largest)


def steps_of(key, shape, shards, least, high):
    factor_of, own = 1.0, jax.random.fold_in(key, 6)
    for dim, blocks in shards:
        steps = jnp.exp(jax.random.uniform(jax.random.fold_in(own, dim), (blocks,), jnp.float32, least / len(shards), high / len(shards)))
        factor_of = factor_of * jnp.repeat(steps, shape[dim] // blocks).reshape([-1 if axis == dim else 1 for axis in range(len(shape))])
    return factor_of


def centred(rng, extent, width, most, cuts=(), held_as=jnp.bfloat16):
    factor_of = steps_of(rng, extent, cuts, -0.22, 0.18) if cuts else 1.0
    drawn = jax.random.normal(rng, extent, jnp.float32) * width * factor_of
    return jnp.minimum(jnp.maximum(drawn, -most), most).astype(held_as)


def setup_inputs(seed: int = 0) -> dict:
    seeds = jax.random.split(jax.random.key(seed), 9)
    return {
        "features": centred(seeds[0], (NODES, F), 1.0, 6.0, ((0, 32),)),
        "seed_rows": place_ends(jax.random.randint(seeds[1], (SEEDS_ALL,), 0, ROWS_DEV), jax.random.fold_in(seeds[1], 1), 0, ROWS_DEV - 1).astype(jnp.int32),
        "hop1_ids": draw_hop1_ids(jax.random.fold_in(seeds[8], 71), 0),
        "hop2_ids": draw_hop2_ids(jax.random.fold_in(seeds[8], 71), 0),
        "w_self": centred(seeds[4], (F, H), F ** -0.5, 0.21875),
        "w_neigh": centred(seeds[5], (F, H), F ** -0.5, 0.21875),
        "bias": centred(seeds[6], (H,), 0.5, 3.0, (), jnp.float32),
        "cotangent": centred(seeds[7], (SEEDS_ALL, H), 1.0, 6.0, ((0, 32),)),
    }


def contract_rows(left, right):
    return lax.dot_general(left.astype(jnp.float32), right.astype(jnp.float32), (((0,), (0,)), ((), ())))


def reference(features, seed_rows, hop1_ids, hop2_ids, w_self, w_neigh, bias, cotangent):
    devices = N_GX * N_GY
    offsets = jnp.arange(devices, dtype=jnp.int32) * ROWS_DEV
    seed_ids = seed_rows.reshape(devices, SEEDS).astype(jnp.int32) + offsets[:, None]
    near_ids = hop1_ids.reshape(devices, SEEDS * K1)
    far_ids = hop2_ids.reshape(devices, SEEDS * K1 * K2)
    cot_parts = cotangent.reshape(devices, SEEDS, H)

    def visit_device(totals, inputs):
        grad_self, grad_neigh, grad_bias = totals
        seed_id, near_id, far_id, cot_part = inputs
        x_seed = features[seed_id]
        x_near = features[near_id]
        far_rows = features[far_id].astype(jnp.float32).reshape(SEEDS * K1, K2, F)
        pooled_far = (jnp.sum(far_rows, axis=1) / K2).astype(jnp.bfloat16)
        pre_near = (jnp.dot(x_near, w_self, preferred_element_type=jnp.float32)
                    + jnp.dot(pooled_far, w_neigh, preferred_element_type=jnp.float32) + bias)
        hidden_near = jnp.maximum(pre_near, 0.0).astype(jnp.bfloat16)
        pooled_near = (jnp.sum(x_near.astype(jnp.float32).reshape(SEEDS, K1, F), axis=1) / K1).astype(jnp.bfloat16)
        pre_seed = (jnp.dot(x_seed, w_self, preferred_element_type=jnp.float32)
                    + jnp.dot(pooled_near, w_neigh, preferred_element_type=jnp.float32) + bias)
        hidden_seed = jnp.maximum(pre_seed, 0.0).astype(jnp.bfloat16)
        summed = hidden_seed.astype(jnp.float32) + jnp.sum(hidden_near.astype(jnp.float32).reshape(SEEDS, K1, H), axis=1)
        embedded = (summed / (1 + K1)).astype(jnp.bfloat16)
        spread = (cot_part.astype(jnp.float32) / (1 + K1)).astype(jnp.bfloat16)
        zero_value = jnp.zeros((), jnp.bfloat16)
        delta_seed = jnp.where(pre_seed > 0, spread, zero_value)
        delta_near = jnp.where(pre_near > 0, jnp.repeat(spread, K1, axis=0), zero_value)
        grad_self = grad_self + contract_rows(x_seed, delta_seed) + contract_rows(x_near, delta_near)
        grad_neigh = grad_neigh + contract_rows(pooled_near, delta_seed) + contract_rows(pooled_far, delta_near)
        grad_bias = (grad_bias + jnp.sum(delta_seed.astype(jnp.float32), axis=0)
                     + jnp.sum(delta_near.astype(jnp.float32), axis=0))
        return (grad_self, grad_neigh, grad_bias), embedded

    starting = (jnp.zeros((F, H), jnp.float32), jnp.zeros((F, H), jnp.float32), jnp.zeros((H,), jnp.float32))
    totals, embedded = lax.scan(visit_device, starting, (seed_ids, near_ids, far_ids, cot_parts))
    return embedded.reshape(SEEDS_ALL, H), totals[0], totals[1], totals[2]
```

```python
import functools

import jax
import jax.numpy as jnp
from jax import lax
from jax.experimental import pallas as pl
from jax.experimental.pallas import tpu as pltpu
from jax.sharding import PartitionSpec as P

MESH = pl.DeviceIdType.MESH


def exchange_kernel(split_x, split_y, x_ref, o_ref, own_sem, send_sem, recv_sem):
    devices = split_x * split_y
    me = lax.axis_index("gx") * split_y + lax.axis_index("gy")

    def copy_to(peer):
        return pltpu.make_async_remote_copy(
            src_ref=x_ref.at[peer],
            dst_ref=o_ref.at[me],
            send_sem=send_sem.at[peer],
            recv_sem=recv_sem.at[me],
            device_id=(peer // split_y, lax.rem(peer, split_y)),
            device_id_type=MESH,
        )

    def copy_from(peer):
        return pltpu.make_async_remote_copy(
            src_ref=x_ref.at[peer],
            dst_ref=o_ref.at[peer],
            send_sem=send_sem.at[peer],
            recv_sem=recv_sem.at[peer],
            device_id=(peer // split_y, lax.rem(peer, split_y)),
            device_id_type=MESH,
        )

    own = pltpu.make_async_copy(x_ref.at[me], o_ref.at[me], own_sem)
    own.start()
    barrier = pltpu.get_barrier_semaphore()

    @pl.loop(1, devices)
    def _(k):
        peer = lax.rem(me + k, devices)
        pl.semaphore_signal(
            barrier,
            inc=1,
            device_id=(peer // split_y, lax.rem(peer, split_y)),
            device_id_type=MESH,
        )

    pl.semaphore_wait(barrier, devices - 1)

    @pl.loop(1, devices)
    def _(k):
        copy_to(lax.rem(me + k, devices)).start()

    @pl.loop(1, devices)
    def _(k):
        copy_from(lax.rem(me + devices - k, devices)).wait_recv()

    @pl.loop(1, devices)
    def _(k):
        copy_to(lax.rem(me + k, devices)).wait_send()

    own.wait()


def exchange(x, split_x, split_y, name, number):
    devices = split_x * split_y
    return pl.pallas_call(
        functools.partial(exchange_kernel, split_x, split_y),
        out_shape=jax.ShapeDtypeStruct(x.shape, x.dtype),
        in_specs=[pl.BlockSpec(memory_space=pl.ANY)],
        out_specs=pl.BlockSpec(memory_space=pl.ANY),
        scratch_shapes=[
            pltpu.SemaphoreType.DMA,
            pltpu.SemaphoreType.DMA((devices,)),
            pltpu.SemaphoreType.DMA((devices,)),
        ],
        compiler_params=pltpu.CompilerParams(collective_id=number, has_side_effects=True),
        name=name,
    )(x)


def one_hot(ids, size):
    return (ids[:, None] == jnp.arange(size, dtype=jnp.int32)[None, :]).astype(jnp.bfloat16)


def matmul(left, right):
    return jnp.dot(left, right, preferred_element_type=jnp.float32)


def body(features, seed_rows, hop1_ids, hop2_ids, w_self, w_neigh, bias, cotangent):
    split_x = lax.axis_size("gx")
    split_y = lax.axis_size("gy")
    devices = split_x * split_y
    rows_dev, width = features.shape
    hidden_width = w_self.shape[1]
    seeds = seed_rows.shape[0]
    fan_one = hop1_ids.shape[1]
    fan_two = hop2_ids.shape[2]
    near_total = seeds * fan_one
    far_total = near_total * fan_two
    near_cap = max(2, 3 * near_total // (2 * devices))
    far_cap = max(2, 3 * far_total // (2 * devices))
    cap = -(-(near_cap + far_cap) // 16) * 16
    lanes = -(-cap // 128) * 128
    bf16 = jnp.bfloat16

    ids = jnp.concatenate([hop2_ids.reshape(-1), hop1_ids.reshape(-1)])
    items = far_total + near_total
    owners = ids // rows_dev
    local = ids - owners * rows_dev
    at = jnp.arange(items, dtype=jnp.int32)
    is_near = at >= far_total
    owned = (jnp.arange(devices, dtype=jnp.int32)[:, None] == owners[None, :]).astype(bf16)
    earlier = ((at[:, None] < at[None, :]) & (is_near[:, None] == is_near[None, :])).astype(bf16)
    ranks = jnp.sum(matmul(owned, earlier) * owned.astype(jnp.float32), axis=0).astype(jnp.int32)
    place = jnp.where(is_near, far_cap, 0) + ranks
    high = (local // 128).astype(bf16)
    low = (local % 128).astype(bf16)
    split_ids = matmul(
        jnp.concatenate([owned * high[None, :], owned * low[None, :]], axis=0), one_hot(place, lanes)
    )
    request = (split_ids[:devices] * 128.0 + split_ids[devices:]).astype(jnp.int32)
    request = jnp.broadcast_to(request[:, None, :], (devices, 8, lanes))
    asked = exchange(request, split_x, split_y, "ask", 0)[:, 0, :cap].reshape(-1)

    served = matmul(one_hot(asked, rows_dev), features).astype(bf16)
    rows = exchange(served.reshape(devices, cap, width), split_x, split_y, "answer", 1)
    rows = rows.reshape(devices * cap, width)

    slots = owners * cap + place
    far_slots = slots[:far_total].reshape(near_total, fan_two)
    near_slots = slots[far_total:]
    column = jnp.arange(devices * cap, dtype=jnp.int32)[None, :]
    far_pick = sum((far_slots[:, j : j + 1] == column).astype(jnp.float32) for j in range(fan_two)).astype(bf16)
    pooled_far = (matmul(far_pick, rows) / fan_two).astype(bf16)
    near_rows = matmul(one_hot(near_slots, devices * cap), rows).astype(bf16)
    seed_x = matmul(one_hot(seed_rows, rows_dev), features).astype(bf16)
    summed_near = jnp.sum(near_rows.astype(jnp.float32).reshape(seeds, fan_one, width), axis=1)
    pooled_near = (summed_near / fan_one).astype(bf16)

    x = jnp.concatenate(
        [
            jnp.concatenate([seed_x, near_rows], axis=0),
            jnp.concatenate([pooled_near, pooled_far], axis=0),
        ],
        axis=1,
    )
    pre = matmul(x, jnp.concatenate([w_self, w_neigh], axis=0)) + bias
    hidden = jnp.maximum(pre, 0.0).astype(bf16).astype(jnp.float32)
    summed = hidden[:seeds] + jnp.sum(hidden[seeds:].reshape(seeds, fan_one, hidden_width), axis=1)
    embedded = (summed / (1 + fan_one)).astype(bf16)
    spread = (cotangent.astype(jnp.float32) / (1 + fan_one)).astype(bf16)
    spread = jnp.concatenate([spread, jnp.repeat(spread, fan_one, axis=0)], axis=0)
    delta = jnp.where(pre > 0, spread, jnp.zeros((), bf16))

    ones = jnp.ones((x.shape[0], 128), bf16)
    shares = lax.dot_general(
        delta,
        jnp.concatenate([x, ones], axis=1),
        (((0,), (0,)), ((), ())),
        preferred_element_type=jnp.float32,
    ).astype(bf16)
    block = hidden_width // devices
    shares = exchange(shares.reshape(devices, block, -1), split_x, split_y, "share", 2)
    total = jnp.sum(shares.astype(jnp.float32), axis=0)
    return (
        embedded,
        total[:, :width].T,
        total[:, width : 2 * width].T,
        total[:, 2 * width],
    )


def solution(mesh):
    in_specs = (
        P(("gx", "gy"), None),
        P(("gx", "gy")),
        P(("gx", "gy"), None),
        P(("gx", "gy"), None, None),
        P(),
        P(),
        P(),
        P(("gx", "gy"), None),
    )
    out_specs = (
        P(("gx", "gy"), None),
        P(None, ("gx", "gy")),
        P(None, ("gx", "gy")),
        P(("gx", "gy")),
    )
    return jax.shard_map(body, mesh=mesh, in_specs=in_specs, out_specs=out_specs, check_vma=False)
```

```python
import functools

import jax
import jax.numpy as jnp
from jax import lax
from jax.experimental import pallas as pl
from jax.experimental.pallas import tpu as pltpu
from jax.sharding import PartitionSpec as P

MESH = pl.DeviceIdType.MESH


def exchange_kernel(wide, count, stride, source, x_ref, o_ref, own_sem, send_sem, recv_sem):
    at_x, at_y = lax.axis_index("gx"), lax.axis_index("gy")
    if stride == 1:
        base = (at_y // count) * count
    else:
        base = lax.rem(at_y, stride)
    members = (lax.axis_size("gx") if wide else 1) * count
    me = (at_x * count if wide else 0) + (at_y - base) // stride

    def coords(peer):
        return (peer // count if wide else at_x, base + stride * lax.rem(peer, count))

    def copy(peer, slot):
        return pltpu.make_async_remote_copy(
            src_ref=source(x_ref, peer),
            dst_ref=o_ref.at[slot],
            send_sem=send_sem.at[peer],
            recv_sem=recv_sem.at[slot],
            device_id=coords(peer),
            device_id_type=MESH,
        )

    own = pltpu.make_async_copy(source(x_ref, me), o_ref.at[me], own_sem)
    own.start()
    barrier = pltpu.get_barrier_semaphore()

    @pl.loop(1, members)
    def _(k):
        peer = lax.rem(me + k, members)
        pl.semaphore_signal(barrier, inc=1, device_id=coords(peer), device_id_type=MESH)

    pl.semaphore_wait(barrier, members - 1)

    @pl.loop(1, members)
    def _(k):
        copy(lax.rem(me + k, members), me).start()

    @pl.loop(1, members)
    def _(k):
        peer = lax.rem(me + members - k, members)
        copy(peer, peer).wait_recv()

    @pl.loop(1, members)
    def _(k):
        copy(lax.rem(me + k, members), me).wait_send()

    own.wait()


def exchange(x, members, block, wide, count, stride, name, number, source=lambda ref, peer: ref.at[peer]):
    return pl.pallas_call(
        functools.partial(exchange_kernel, wide, count, stride, source),
        out_shape=jax.ShapeDtypeStruct((members, *block), x.dtype),
        in_specs=[pl.BlockSpec(memory_space=pl.ANY)],
        out_specs=pl.BlockSpec(memory_space=pl.ANY),
        scratch_shapes=[
            pltpu.SemaphoreType.DMA,
            pltpu.SemaphoreType.DMA((members,)),
            pltpu.SemaphoreType.DMA((members,)),
        ],
        compiler_params=pltpu.CompilerParams(collective_id=number, has_side_effects=True),
        name=name,
    )(x)


def one_hot(ids, size):
    return (ids[:, None] == jnp.arange(size, dtype=jnp.int32)[None, :]).astype(jnp.bfloat16)


def matmul(left, right):
    return jnp.dot(left, right, preferred_element_type=jnp.float32)


def body(features, seed_rows, hop1_ids, hop2_ids, w_self, w_neigh, bias, cotangent):
    split_x = lax.axis_size("gx")
    split_y = lax.axis_size("gy")
    devices = split_x * split_y
    rows_dev, width = features.shape
    hidden_width = w_self.shape[1]
    seeds = seed_rows.shape[0]
    fan_one = hop1_ids.shape[1]
    fan_two = hop2_ids.shape[2]
    near_total = seeds * fan_one
    far_total = near_total * fan_two
    near_cap = max(2, 3 * near_total // (2 * devices))
    far_cap = max(2, 3 * far_total // (2 * devices))
    cap = -(-(near_cap + far_cap) // 16) * 16
    lanes = -(-cap // 128) * 128
    bf16 = jnp.bfloat16

    half_y = split_y // 2
    half = split_x * half_y
    at_half = lax.axis_index("gy") // half_y
    mirror = lax.ppermute(features, "gy", [(i, (i + half_y) % split_y) for i in range(split_y)])

    ids = jnp.concatenate([hop2_ids.reshape(-1), hop1_ids.reshape(-1)])
    items = far_total + near_total
    holders = ids // rows_dev
    local = ids - holders * rows_dev
    held_y = holders % split_y
    other = (held_y // half_y != at_half).astype(jnp.int32)
    owners = other * half + (holders // split_y) * half_y + held_y % half_y
    at = jnp.arange(items, dtype=jnp.int32)
    is_near = at >= far_total
    owned = (jnp.arange(devices, dtype=jnp.int32)[:, None] == owners[None, :]).astype(bf16)
    earlier = ((at[:, None] < at[None, :]) & (is_near[:, None] == is_near[None, :])).astype(bf16)
    ranks = jnp.sum(matmul(owned, earlier) * owned.astype(jnp.float32), axis=0).astype(jnp.int32)
    place = jnp.where(is_near, far_cap, 0) + ranks
    high = (local // 128).astype(bf16)
    low = (local % 128).astype(bf16)
    split_ids = matmul(
        jnp.concatenate([owned * high[None, :], owned * low[None, :]], axis=0), one_hot(place, lanes)
    )
    request = (split_ids[:devices] * 128.0 + split_ids[devices:]).astype(jnp.int32)
    request = request.reshape(2, half, lanes).transpose(1, 0, 2)
    request = jnp.concatenate([request] * 4, axis=1)
    asked = exchange(request, half, (8, lanes), True, half_y, 1, "ask", 0)

    slots = owners * cap + place
    far_slots = slots[:far_total].reshape(near_total, fan_two)
    near_slots = slots[far_total:]
    picked = 0.0
    for side, table in enumerate((features, mirror)):
        served = matmul(one_hot(asked[:, side, :cap].reshape(-1), rows_dev), table).astype(bf16)
        served = served.reshape(half, cap, width)
        rows = exchange(served, half, (cap, width), True, half_y, 1, f"answer{side}", 1 + side)
        column = jnp.arange(half * cap, dtype=jnp.int32)[None, :] + side * half * cap
        far_pick = sum((far_slots[:, j : j + 1] == column).astype(jnp.float32) for j in range(fan_two))
        near_pick = (near_slots[:, None] == column).astype(bf16)
        pick = jnp.concatenate([near_pick, far_pick.astype(bf16)], axis=0)
        picked = picked + matmul(pick, rows.reshape(half * cap, width))
    near_rows = picked[:near_total].astype(bf16)
    pooled_far = (picked[near_total:] / fan_two).astype(bf16)
    seed_x = matmul(one_hot(seed_rows, rows_dev), features).astype(bf16)
    summed_near = jnp.sum(near_rows.astype(jnp.float32).reshape(seeds, fan_one, width), axis=1)
    pooled_near = (summed_near / fan_one).astype(bf16)

    x = jnp.concatenate(
        [
            jnp.concatenate([seed_x, near_rows], axis=0),
            jnp.concatenate([pooled_near, pooled_far], axis=0),
        ],
        axis=1,
    )
    pre = matmul(x, jnp.concatenate([w_self, w_neigh], axis=0)) + bias
    hidden = jnp.maximum(pre, 0.0).astype(bf16).astype(jnp.float32)
    summed = hidden[:seeds] + jnp.sum(hidden[seeds:].reshape(seeds, fan_one, hidden_width), axis=1)
    embedded = (summed / (1 + fan_one)).astype(bf16)
    spread = (cotangent.astype(jnp.float32) / (1 + fan_one)).astype(bf16)
    spread = jnp.concatenate([spread, jnp.repeat(spread, fan_one, axis=0)], axis=0)
    delta = jnp.where(pre > 0, spread, jnp.zeros((), bf16))

    ones = jnp.ones((x.shape[0], 128), bf16)
    shares = lax.dot_general(
        delta,
        jnp.concatenate([x, ones], axis=1),
        (((0,), (0,)), ((), ())),
        preferred_element_type=jnp.float32,
    ).astype(bf16)
    block = hidden_width // devices
    pair = 2
    depth = split_y // pair
    plane = split_x * pair
    shares = exchange(
        shares.reshape(split_x, depth, pair, block, -1),
        plane,
        (depth, block, shares.shape[1]),
        True,
        pair,
        1,
        "share",
        3,
        lambda ref, peer: ref.at[peer // pair, :, lax.rem(peer, pair)],
    )
    shares = jnp.sum(shares.astype(jnp.float32), axis=0).astype(bf16)
    shares = exchange(shares, depth, shares.shape[1:], False, depth, pair, "share_along", 4)
    total = jnp.sum(shares.astype(jnp.float32), axis=0)
    return (
        embedded,
        total[:, :width].T,
        total[:, width : 2 * width].T,
        total[:, 2 * width],
    )


def solution(mesh):
    in_specs = (
        P(("gx", "gy"), None),
        P(("gx", "gy")),
        P(("gx", "gy"), None),
        P(("gx", "gy"), None, None),
        P(),
        P(),
        P(),
        P(("gx", "gy"), None),
    )
    out_specs = (
        P(("gx", "gy"), None),
        P(None, ("gx", "gy")),
        P(None, ("gx", "gy")),
        P(("gx", "gy")),
    )
    return jax.shard_map(body, mesh=mesh, in_specs=in_specs, out_specs=out_specs, check_vma=False)
```

```python
import functools

import jax
import jax.numpy as jnp
from jax import lax
from jax.experimental import pallas as pl
from jax.experimental.pallas import tpu as pltpu
from jax.sharding import PartitionSpec as P

MESH = pl.DeviceIdType.MESH


def exchange_kernel(wide, count, stride, source, keep, x_ref, o_ref, own_sem, send_sem, recv_sem):
    at_x, at_y = lax.axis_index("gx"), lax.axis_index("gy")
    if stride == 1:
        base = (at_y // count) * count
    else:
        base = lax.rem(at_y, stride)
    members = (lax.axis_size("gx") if wide else 1) * count
    me = (at_x * count if wide else 0) + (at_y - base) // stride

    def coords(peer):
        return (peer // count if wide else at_x, base + stride * lax.rem(peer, count))

    def copy(peer, slot):
        return pltpu.make_async_remote_copy(
            src_ref=source(x_ref, peer),
            dst_ref=o_ref.at[slot],
            send_sem=send_sem.at[peer],
            recv_sem=recv_sem.at[slot],
            device_id=coords(peer),
            device_id_type=MESH,
        )

    if keep:
        own = pltpu.make_async_copy(source(x_ref, me), o_ref.at[me], own_sem)
        own.start()
    barrier = pltpu.get_barrier_semaphore()

    @pl.loop(1, members)
    def _(k):
        peer = lax.rem(me + k, members)
        pl.semaphore_signal(barrier, inc=1, device_id=coords(peer), device_id_type=MESH)

    pl.semaphore_wait(barrier, members - 1)

    @pl.loop(1, members)
    def _(k):
        copy(lax.rem(me + k, members), me if keep else 0).start()

    @pl.loop(1, members)
    def _(k):
        peer = lax.rem(me + members - k, members)
        copy(peer, peer if keep else 0).wait_recv()

    @pl.loop(1, members)
    def _(k):
        copy(lax.rem(me + k, members), me if keep else 0).wait_send()

    if keep:
        own.wait()


def exchange(
    x, members, block, wide, count, stride, name, number, source=lambda ref, peer: ref.at[peer], keep=True
):
    return pl.pallas_call(
        functools.partial(exchange_kernel, wide, count, stride, source, keep),
        out_shape=jax.ShapeDtypeStruct((members if keep else 1, *block), x.dtype),
        in_specs=[pl.BlockSpec(memory_space=pl.ANY)],
        out_specs=pl.BlockSpec(memory_space=pl.ANY),
        scratch_shapes=[
            pltpu.SemaphoreType.DMA,
            pltpu.SemaphoreType.DMA((members,)),
            pltpu.SemaphoreType.DMA((members,)),
        ],
        compiler_params=pltpu.CompilerParams(collective_id=number, has_side_effects=True),
        name=name,
    )(x)


def one_hot(ids, size):
    return (ids[:, None] == jnp.arange(size, dtype=jnp.int32)[None, :]).astype(jnp.bfloat16)


def matmul(left, right):
    return jnp.dot(left, right, preferred_element_type=jnp.float32)


def body(features, seed_rows, hop1_ids, hop2_ids, w_self, w_neigh, bias, cotangent):
    split_x = lax.axis_size("gx")
    split_y = lax.axis_size("gy")
    devices = split_x * split_y
    rows_dev, width = features.shape
    hidden_width = w_self.shape[1]
    seeds = seed_rows.shape[0]
    fan_one = hop1_ids.shape[1]
    fan_two = hop2_ids.shape[2]
    near_total = seeds * fan_one
    far_total = near_total * fan_two
    near_cap = max(2, 3 * near_total // (2 * devices))
    far_cap = max(2, 3 * far_total // (2 * devices))
    cap = -(-(near_cap + far_cap) // 16) * 16
    lanes = -(-cap // 128) * 128
    bf16 = jnp.bfloat16

    half_y = split_y // 2
    half = split_x * half_y
    at_half = lax.axis_index("gy") // half_y

    ids = jnp.concatenate([hop2_ids.reshape(-1), hop1_ids.reshape(-1)])
    items = far_total + near_total
    holders = ids // rows_dev
    local = ids - holders * rows_dev
    held_y = holders % split_y
    other = (held_y // half_y != at_half).astype(jnp.int32)
    owners = other * half + (holders // split_y) * half_y + held_y % half_y
    at = jnp.arange(items, dtype=jnp.int32)
    is_near = at >= far_total
    owned = (jnp.arange(devices, dtype=jnp.int32)[:, None] == owners[None, :]).astype(bf16)
    earlier = ((at[:, None] < at[None, :]) & (is_near[:, None] == is_near[None, :])).astype(bf16)
    ranks = jnp.sum(matmul(owned, earlier) * owned.astype(jnp.float32), axis=0).astype(jnp.int32)
    place = jnp.where(is_near, far_cap, 0) + ranks
    high = (local // 128).astype(bf16)
    low = (local % 128).astype(bf16)
    split_ids = matmul(
        jnp.concatenate([owned * high[None, :], owned * low[None, :]], axis=0), one_hot(place, lanes)
    )
    request = (split_ids[:devices] * 128.0 + split_ids[devices:]).astype(jnp.int32)
    request = request.reshape(2, half, lanes).transpose(1, 0, 2)
    request = jnp.concatenate([request] * 4, axis=1)
    asked = exchange(request, half, (8, lanes), True, half_y, 1, "ask", 0)

    asked, sent = lax.optimization_barrier((asked, features))
    mirror = lax.ppermute(sent, "gy", [(i, (i + half_y) % split_y) for i in range(split_y)])

    slots = owners * cap + place
    far_slots = slots[:far_total].reshape(near_total, fan_two)
    near_slots = slots[far_total:]
    picked = 0.0
    for side, table in enumerate((features, mirror)):
        served = matmul(one_hot(asked[:, side, :cap].reshape(-1), rows_dev), table).astype(bf16)
        served = served.reshape(half, cap, width)
        rows = exchange(served, half, (cap, width), True, half_y, 1, f"answer{side}", 1 + side)
        column = jnp.arange(half * cap, dtype=jnp.int32)[None, :] + side * half * cap
        far_pick = sum((far_slots[:, j : j + 1] == column).astype(jnp.float32) for j in range(fan_two))
        near_pick = (near_slots[:, None] == column).astype(bf16)
        pick = jnp.concatenate([near_pick, far_pick.astype(bf16)], axis=0)
        picked = picked + matmul(pick, rows.reshape(half * cap, width))
    near_rows = picked[:near_total].astype(bf16)
    pooled_far = (picked[near_total:] / fan_two).astype(bf16)
    seed_x = matmul(one_hot(seed_rows, rows_dev), features).astype(bf16)
    summed_near = jnp.sum(near_rows.astype(jnp.float32).reshape(seeds, fan_one, width), axis=1)
    pooled_near = (summed_near / fan_one).astype(bf16)

    x = jnp.concatenate(
        [
            jnp.concatenate([seed_x, near_rows], axis=0),
            jnp.concatenate([pooled_near, pooled_far], axis=0),
        ],
        axis=1,
    )
    pre = matmul(x, jnp.concatenate([w_self, w_neigh], axis=0)) + bias
    hidden = jnp.maximum(pre, 0.0).astype(bf16).astype(jnp.float32)
    summed = hidden[:seeds] + jnp.sum(hidden[seeds:].reshape(seeds, fan_one, hidden_width), axis=1)
    embedded = (summed / (1 + fan_one)).astype(bf16)
    spread = (cotangent.astype(jnp.float32) / (1 + fan_one)).astype(bf16)
    spread = jnp.concatenate([spread, jnp.repeat(spread, fan_one, axis=0)], axis=0)
    delta = jnp.where(pre > 0, spread, jnp.zeros((), bf16))

    ones = jnp.ones((x.shape[0], 128), bf16)
    shares = lax.dot_general(
        delta,
        jnp.concatenate([x, ones], axis=1),
        (((0,), (0,)), ((), ())),
        preferred_element_type=jnp.float32,
    ).astype(bf16)
    block = hidden_width // devices
    pair = 2
    depth = split_y // pair
    shares = shares.reshape(split_x, depth, pair, block, -1)
    tail = (depth, block, shares.shape[-1])
    given = exchange(
        shares,
        pair,
        (split_x, *tail),
        False,
        pair,
        1,
        "share_pair",
        3,
        lambda ref, peer: ref.at[:, :, peer],
        keep=False,
    )[0]
    kept = lax.dynamic_index_in_dim(shares, lax.axis_index("gy") % pair, 2, keepdims=False)
    shares = (kept.astype(jnp.float32) + given.astype(jnp.float32)).astype(bf16)
    shares = exchange(shares, split_x, tail, True, 1, 1, "share_across", 5)
    shares = jnp.sum(shares.astype(jnp.float32), axis=0).astype(bf16)
    shares = exchange(shares, depth, shares.shape[1:], False, depth, pair, "share_along", 4)
    total = jnp.sum(shares.astype(jnp.float32), axis=0)
    return (
        embedded,
        total[:, :width].T,
        total[:, width : 2 * width].T,
        total[:, 2 * width],
    )


def solution(mesh):
    in_specs = (
        P(("gx", "gy"), None),
        P(("gx", "gy")),
        P(("gx", "gy"), None),
        P(("gx", "gy"), None, None),
        P(),
        P(),
        P(),
        P(("gx", "gy"), None),
    )
    out_specs = (
        P(("gx", "gy"), None),
        P(None, ("gx", "gy")),
        P(None, ("gx", "gy")),
        P(("gx", "gy")),
    )
    return jax.shard_map(body, mesh=mesh, in_specs=in_specs, out_specs=out_specs, check_vma=False)
```

```python
import functools

import jax
import jax.numpy as jnp
from jax import lax
from jax.experimental import pallas as pl
from jax.experimental.pallas import tpu as pltpu
from jax.sharding import PartitionSpec as P


MESH = pl.DeviceIdType.MESH


def exchange_kernel(wide, count, stride, source, keep, x_ref, o_ref, own_sem, send_sem, recv_sem):
    at_x, at_y = lax.axis_index("gx"), lax.axis_index("gy")
    if stride == 1:
        base = (at_y // count) * count
    else:
        base = lax.rem(at_y, stride)
    members = (lax.axis_size("gx") if wide else 1) * count
    me = (at_x * count if wide else 0) + (at_y - base) // stride

    def coords(peer):
        return (peer // count if wide else at_x, base + stride * lax.rem(peer, count))

    def copy(peer, slot):
        return pltpu.make_async_remote_copy(
            src_ref=source(x_ref, peer),
            dst_ref=o_ref.at[slot],
            send_sem=send_sem.at[peer],
            recv_sem=recv_sem.at[slot],
            device_id=coords(peer),
            device_id_type=MESH,
        )

    if keep:
        own = pltpu.make_async_copy(source(x_ref, me), o_ref.at[me], own_sem)
        own.start()
    barrier = pltpu.get_barrier_semaphore()

    @pl.loop(1, members)
    def _(k):
        peer = lax.rem(me + k, members)
        pl.semaphore_signal(barrier, inc=1, device_id=coords(peer), device_id_type=MESH)

    pl.semaphore_wait(barrier, members - 1)

    @pl.loop(1, members)
    def _(k):
        copy(lax.rem(me + k, members), me if keep else 0).start()

    @pl.loop(1, members)
    def _(k):
        peer = lax.rem(me + members - k, members)
        copy(peer, peer if keep else 0).wait_recv()

    @pl.loop(1, members)
    def _(k):
        copy(lax.rem(me + k, members), me if keep else 0).wait_send()

    if keep:
        own.wait()


def exchange(
    x, members, block, wide, count, stride, number, source=lambda ref, peer: ref.at[peer], keep=True
):
    return pl.pallas_call(
        functools.partial(exchange_kernel, wide, count, stride, source, keep),
        out_shape=jax.ShapeDtypeStruct((members if keep else 1, *block), x.dtype),
        in_specs=[pl.BlockSpec(memory_space=pl.ANY)],
        out_specs=pl.BlockSpec(memory_space=pl.ANY),
        scratch_shapes=[
            pltpu.SemaphoreType.DMA,
            pltpu.SemaphoreType.DMA((members,)),
            pltpu.SemaphoreType.DMA((members,)),
        ],
        compiler_params=pltpu.CompilerParams(collective_id=number, has_side_effects=True),
    )(x)


def one_hot(ids, size):
    return (ids[:, None] == jnp.arange(size, dtype=jnp.int32)[None, :]).astype(jnp.bfloat16)


def matmul(left, right):
    return jnp.dot(left, right, preferred_element_type=jnp.float32)


def body(features, seed_rows, hop1_ids, hop2_ids, w_self, w_neigh, bias, cotangent):
    split_x = lax.axis_size("gx")
    split_y = lax.axis_size("gy")
    devices = split_x * split_y
    rows_dev, width = features.shape
    hidden_width = w_self.shape[1]
    seeds = seed_rows.shape[0]
    fan_one = hop1_ids.shape[1]
    fan_two = hop2_ids.shape[2]
    near_total = seeds * fan_one
    far_total = near_total * fan_two
    near_cap = max(2, 3 * near_total // (2 * devices))
    far_cap = max(2, 3 * far_total // (2 * devices))
    cap = -(-(near_cap + far_cap) // 16) * 16
    lanes = -(-cap // 128) * 128
    bf16 = jnp.bfloat16

    half_y = split_y // 2
    half = split_x * half_y
    at_half = lax.axis_index("gy") // half_y

    ids = jnp.concatenate([hop2_ids.reshape(-1), hop1_ids.reshape(-1)])
    items = far_total + near_total
    holders = ids // rows_dev
    local = ids - holders * rows_dev
    held_y = holders % split_y
    other = (held_y // half_y != at_half).astype(jnp.int32)
    owners = other * half + (holders // split_y) * half_y + held_y % half_y
    at = jnp.arange(items, dtype=jnp.int32)
    is_near = at >= far_total
    owned = (jnp.arange(devices, dtype=jnp.int32)[:, None] == owners[None, :]).astype(bf16)
    earlier = ((at[:, None] < at[None, :]) & (is_near[:, None] == is_near[None, :])).astype(bf16)
    ranks = jnp.sum(matmul(owned, earlier) * owned.astype(jnp.float32), axis=0).astype(jnp.int32)
    place = jnp.where(is_near, far_cap, 0) + ranks
    high = (local // 128).astype(bf16)
    low = (local % 128).astype(bf16)
    split_ids = matmul(
        jnp.concatenate([owned * high[None, :], owned * low[None, :]], axis=0), one_hot(place, lanes)
    )
    request = (split_ids[:devices] * 128.0 + split_ids[devices:]).astype(jnp.int32)
    request = request.reshape(2, half, lanes).transpose(1, 0, 2)
    request = jnp.concatenate([request] * 4, axis=1)
    asked = exchange(request, half, (8, lanes), True, half_y, 1, 0)

    first = max(128, 2 * width // 3 // 128 * 128)
    over = [(i, (i + half_y) % split_y) for i in range(split_y)]
    asked, sent = lax.optimization_barrier((asked, features[:, :first]))
    mirror_first = lax.ppermute(sent, "gy", over)

    slots = owners * cap + place
    far_slots = slots[:far_total].reshape(near_total, fan_two)
    near_slots = slots[far_total:]

    def pick(side):
        column = jnp.arange(half * cap, dtype=jnp.int32)[None, :] + side * half * cap
        far_pick = sum((far_slots[:, j : j + 1] == column).astype(jnp.float32) for j in range(fan_two))
        near_pick = (near_slots[:, None] == column).astype(bf16)
        return jnp.concatenate([near_pick, far_pick.astype(bf16)], axis=0)

    def answer(asked, side, table, number):
        columns = table.shape[1]
        served = matmul(one_hot(asked[:, side, :cap].reshape(-1), rows_dev), table).astype(bf16)
        rows = exchange(
            served.reshape(half, cap, columns), half, (cap, columns), True, half_y, 1, number
        )
        return rows.reshape(half * cap, columns)

    rows_own = answer(asked, 0, features, 1)
    rows_own, sent = lax.optimization_barrier((rows_own, features[:, first:]))
    mirror_last = lax.ppermute(sent, "gy", over)
    rows_first = answer(asked, 1, mirror_first, 2)
    rows_first, asked = lax.optimization_barrier((rows_first, asked))
    rows_last = answer(asked, 1, mirror_last, 6)
    picked = matmul(pick(0), rows_own) + jnp.concatenate(
        [matmul(pick(1), rows_first), matmul(pick(1), rows_last)], axis=1
    )
    near_rows = picked[:near_total].astype(bf16)
    pooled_far = (picked[near_total:] / fan_two).astype(bf16)
    seed_x = matmul(one_hot(seed_rows, rows_dev), features).astype(bf16)
    summed_near = jnp.sum(near_rows.astype(jnp.float32).reshape(seeds, fan_one, width), axis=1)
    pooled_near = (summed_near / fan_one).astype(bf16)

    x = jnp.concatenate(
        [
            jnp.concatenate([seed_x, near_rows], axis=0),
            jnp.concatenate([pooled_near, pooled_far], axis=0),
        ],
        axis=1,
    )
    pre = matmul(x, jnp.concatenate([w_self, w_neigh], axis=0)) + bias
    hidden = jnp.maximum(pre, 0.0).astype(bf16).astype(jnp.float32)
    summed = hidden[:seeds] + jnp.sum(hidden[seeds:].reshape(seeds, fan_one, hidden_width), axis=1)
    embedded = (summed / (1 + fan_one)).astype(bf16)
    spread = (cotangent.astype(jnp.float32) / (1 + fan_one)).astype(bf16)
    spread = jnp.concatenate([spread, jnp.repeat(spread, fan_one, axis=0)], axis=0)
    delta = jnp.where(pre > 0, spread, jnp.zeros((), bf16))

    ones = jnp.ones((x.shape[0], 128), bf16)
    shares = lax.dot_general(
        delta,
        jnp.concatenate([x, ones], axis=1),
        (((0,), (0,)), ((), ())),
        preferred_element_type=jnp.float32,
    ).astype(bf16)
    block = hidden_width // devices
    pair = 2
    depth = split_y // pair
    shares = shares.reshape(split_x, depth, pair, block, -1)
    tail = (depth, block, shares.shape[-1])
    given = exchange(
        shares,
        pair,
        (split_x, *tail),
        False,
        pair,
        1,
        3,
        lambda ref, peer: ref.at[:, :, peer],
        keep=False,
    )[0]
    kept = lax.dynamic_index_in_dim(shares, lax.axis_index("gy") % pair, 2, keepdims=False)
    shares = (kept.astype(jnp.float32) + given.astype(jnp.float32)).astype(bf16)
    shares = exchange(shares, split_x, tail, True, 1, 1, 5)
    shares = jnp.sum(shares.astype(jnp.float32), axis=0).astype(bf16)
    shares = exchange(shares, depth, shares.shape[1:], False, depth, pair, 4)
    total = jnp.sum(shares.astype(jnp.float32), axis=0)
    return (
        embedded,
        total[:, :width].T,
        total[:, width : 2 * width].T,
        total[:, 2 * width],
    )


def solution(mesh):
    in_specs = (
        P(("gx", "gy"), None),
        P(("gx", "gy")),
        P(("gx", "gy"), None),
        P(("gx", "gy"), None, None),
        P(),
        P(),
        P(),
        P(("gx", "gy"), None),
    )
    out_specs = (
        P(("gx", "gy"), None),
        P(None, ("gx", "gy")),
        P(None, ("gx", "gy")),
        P(("gx", "gy")),
    )

    return jax.shard_map(body, mesh=mesh, in_specs=in_specs, out_specs=out_specs, check_vma=False)
```

```python
import functools

import jax
import jax.numpy as jnp
from jax import lax
from jax.experimental import pallas as pl
from jax.experimental.pallas import tpu as pltpu
from jax.sharding import PartitionSpec as P


MESH = pl.DeviceIdType.MESH


def exchange_kernel(wide, count, stride, source, keep, x_ref, o_ref, own_sem, send_sem, recv_sem):
    at_x, at_y = lax.axis_index("gx"), lax.axis_index("gy")
    if stride == 1:
        base = (at_y // count) * count
    else:
        base = lax.rem(at_y, stride)
    members = (lax.axis_size("gx") if wide else 1) * count
    me = (at_x * count if wide else 0) + (at_y - base) // stride

    def coords(peer):
        return (peer // count if wide else at_x, base + stride * lax.rem(peer, count))

    def copy(peer, slot):
        return pltpu.make_async_remote_copy(
            src_ref=source(x_ref, peer),
            dst_ref=o_ref.at[slot],
            send_sem=send_sem.at[peer],
            recv_sem=recv_sem.at[slot],
            device_id=coords(peer),
            device_id_type=MESH,
        )

    if keep:
        own = pltpu.make_async_copy(source(x_ref, me), o_ref.at[me], own_sem)
        own.start()
    barrier = pltpu.get_barrier_semaphore()

    @pl.loop(1, members)
    def _(k):
        peer = lax.rem(me + k, members)
        pl.semaphore_signal(barrier, inc=1, device_id=coords(peer), device_id_type=MESH)

    pl.semaphore_wait(barrier, members - 1)

    @pl.loop(1, members)
    def _(k):
        copy(lax.rem(me + k, members), me if keep else 0).start()

    @pl.loop(1, members)
    def _(k):
        peer = lax.rem(me + members - k, members)
        copy(peer, peer if keep else 0).wait_recv()

    @pl.loop(1, members)
    def _(k):
        copy(lax.rem(me + k, members), me if keep else 0).wait_send()

    if keep:
        own.wait()


def exchange(
    x, members, block, wide, count, stride, number, source=lambda ref, peer: ref.at[peer], keep=True
):
    return pl.pallas_call(
        functools.partial(exchange_kernel, wide, count, stride, source, keep),
        out_shape=jax.ShapeDtypeStruct((members if keep else 1, *block), x.dtype),
        in_specs=[pl.BlockSpec(memory_space=pl.ANY)],
        out_specs=pl.BlockSpec(memory_space=pl.ANY),
        scratch_shapes=[
            pltpu.SemaphoreType.DMA,
            pltpu.SemaphoreType.DMA((members,)),
            pltpu.SemaphoreType.DMA((members,)),
        ],
        compiler_params=pltpu.CompilerParams(collective_id=number, has_side_effects=True),
    )(x)


def one_hot(ids, size):
    return (ids[:, None] == jnp.arange(size, dtype=jnp.int32)[None, :]).astype(jnp.bfloat16)


def matmul(left, right):
    return jnp.dot(left, right, preferred_element_type=jnp.float32)


def body(features, seed_rows, hop1_ids, hop2_ids, w_self, w_neigh, bias, cotangent):
    split_x = lax.axis_size("gx")
    split_y = lax.axis_size("gy")
    devices = split_x * split_y
    rows_dev, width = features.shape
    hidden_width = w_self.shape[1]
    seeds = seed_rows.shape[0]
    fan_one = hop1_ids.shape[1]
    fan_two = hop2_ids.shape[2]
    near_total = seeds * fan_one
    far_total = near_total * fan_two
    near_cap = max(2, 3 * near_total // (2 * devices))
    far_cap = max(2, 3 * far_total // (2 * devices))
    cap = -(-(near_cap + far_cap) // 16) * 16
    lanes = -(-cap // 128) * 128
    bf16 = jnp.bfloat16

    half_y = split_y // 2
    half = split_x * half_y
    over = [(i, (i + half_y) % split_y) for i in range(split_y)]
    early = max(128, width // 6 // 128 * 128)
    first = max(2 * early, 2 * width // 3 // 128 * 128)
    mirror_early = lax.ppermute(features[:, :early], "gy", over)
    at_half = lax.axis_index("gy") // half_y

    ids = jnp.concatenate([hop2_ids.reshape(-1), hop1_ids.reshape(-1)])
    items = far_total + near_total
    holders = ids // rows_dev
    local = ids - holders * rows_dev
    held_y = holders % split_y
    other = (held_y // half_y != at_half).astype(jnp.int32)
    owners = other * half + (holders // split_y) * half_y + held_y % half_y
    at = jnp.arange(items, dtype=jnp.int32)
    is_near = at >= far_total
    owned = (jnp.arange(devices, dtype=jnp.int32)[:, None] == owners[None, :]).astype(bf16)
    earlier = ((at[:, None] < at[None, :]) & (is_near[:, None] == is_near[None, :])).astype(bf16)
    ranks = jnp.sum(matmul(owned, earlier) * owned.astype(jnp.float32), axis=0).astype(jnp.int32)
    place = jnp.where(is_near, far_cap, 0) + ranks
    high = (local // 128).astype(bf16)
    low = (local % 128).astype(bf16)
    split_ids = matmul(
        jnp.concatenate([owned * high[None, :], owned * low[None, :]], axis=0), one_hot(place, lanes)
    )
    request = (split_ids[:devices] * 128.0 + split_ids[devices:]).astype(jnp.int32)
    request = request.reshape(2, half, lanes).transpose(1, 0, 2)
    request = jnp.concatenate([request] * 4, axis=1)
    asked = exchange(request, half, (8, lanes), True, half_y, 1, 0)

    slots = owners * cap + place
    asked, sent, slots = lax.optimization_barrier((asked, features[:, early:first], slots))
    mirror_first = lax.ppermute(sent, "gy", over)

    far_slots = slots[:far_total].reshape(near_total, fan_two)
    near_slots = slots[far_total:]

    def pick(side):
        column = jnp.arange(half * cap, dtype=jnp.int32)[None, :] + side * half * cap
        far_pick = sum((far_slots[:, j : j + 1] == column).astype(jnp.float32) for j in range(fan_two))
        near_pick = (near_slots[:, None] == column).astype(bf16)
        return jnp.concatenate([near_pick, far_pick.astype(bf16)], axis=0)

    def answer(asked, side, table, number):
        columns = table.shape[1]
        served = matmul(one_hot(asked[:, side, :cap].reshape(-1), rows_dev), table).astype(bf16)
        rows = exchange(
            served.reshape(half, cap, columns), half, (cap, columns), True, half_y, 1, number
        )
        return rows.reshape(half * cap, columns)

    asked, picks = lax.optimization_barrier((asked, (pick(0), pick(1))))
    rows_own = answer(asked, 0, features, 1)
    rows_own, sent = lax.optimization_barrier((rows_own, features[:, first:]))
    mirror_last = lax.ppermute(sent, "gy", over)
    rows_first = answer(asked, 1, jnp.concatenate([mirror_early, mirror_first], axis=1), 2)
    rows_first, asked = lax.optimization_barrier((rows_first, asked))
    rows_last = answer(asked, 1, mirror_last, 6)
    picked = matmul(picks[0], rows_own) + jnp.concatenate(
        [matmul(picks[1], rows_first), matmul(picks[1], rows_last)], axis=1
    )
    near_rows = picked[:near_total].astype(bf16)
    pooled_far = (picked[near_total:] / fan_two).astype(bf16)
    seed_x = matmul(one_hot(seed_rows, rows_dev), features).astype(bf16)
    summed_near = jnp.sum(near_rows.astype(jnp.float32).reshape(seeds, fan_one, width), axis=1)
    pooled_near = (summed_near / fan_one).astype(bf16)

    x = jnp.concatenate(
        [
            jnp.concatenate([seed_x, near_rows], axis=0),
            jnp.concatenate([pooled_near, pooled_far], axis=0),
        ],
        axis=1,
    )
    pre = matmul(x, jnp.concatenate([w_self, w_neigh], axis=0)) + bias
    hidden = jnp.maximum(pre, 0.0).astype(bf16).astype(jnp.float32)
    summed = hidden[:seeds] + jnp.sum(hidden[seeds:].reshape(seeds, fan_one, hidden_width), axis=1)
    embedded = (summed / (1 + fan_one)).astype(bf16)
    spread = (cotangent.astype(jnp.float32) / (1 + fan_one)).astype(bf16)
    spread = jnp.concatenate([spread, jnp.repeat(spread, fan_one, axis=0)], axis=0)
    delta = jnp.where(pre > 0, spread, jnp.zeros((), bf16))

    ones = jnp.ones((x.shape[0], 128), bf16)
    shares = lax.dot_general(
        delta,
        jnp.concatenate([x, ones], axis=1),
        (((0,), (0,)), ((), ())),
        preferred_element_type=jnp.float32,
    ).astype(bf16)
    block = hidden_width // devices
    pair = 2
    depth = split_y // pair
    shares = shares.reshape(split_x, depth, pair, block, -1)
    tail = (depth, block, shares.shape[-1])
    given = exchange(
        shares,
        pair,
        (split_x, *tail),
        False,
        pair,
        1,
        3,
        lambda ref, peer: ref.at[:, :, peer],
        keep=False,
    )[0]
    kept = lax.dynamic_index_in_dim(shares, lax.axis_index("gy") % pair, 2, keepdims=False)
    shares = (kept.astype(jnp.float32) + given.astype(jnp.float32)).astype(bf16)
    shares = exchange(shares, split_x, tail, True, 1, 1, 5)
    shares = jnp.sum(shares.astype(jnp.float32), axis=0).astype(bf16)
    shares = exchange(shares, depth, shares.shape[1:], False, depth, pair, 4)
    total = jnp.sum(shares.astype(jnp.float32), axis=0)
    return (
        embedded,
        total[:, :width].T,
        total[:, width : 2 * width].T,
        total[:, 2 * width],
    )


def solution(mesh):
    in_specs = (
        P(("gx", "gy"), None),
        P(("gx", "gy")),
        P(("gx", "gy"), None),
        P(("gx", "gy"), None, None),
        P(),
        P(),
        P(),
        P(("gx", "gy"), None),
    )
    out_specs = (
        P(("gx", "gy"), None),
        P(None, ("gx", "gy")),
        P(None, ("gx", "gy")),
        P(("gx", "gy")),
    )

    return jax.shard_map(body, mesh=mesh, in_specs=in_specs, out_specs=out_specs, check_vma=False)
```
